32 devices in a mesh: grp: 2 (over x), seq: 8 (over z, y), head: 2 (over core).
Axes of the slice: x: 2, y: 2, z: 4, core: 2. Of those that a mesh axis runs over, the one named last changes fastest.
Arguments:
- query: bfloat16 [2048, 4096], P(('grp', 'seq'), 'head'), parts along dimension 0, may hold values from -6 to 6
- keys: bfloat16 [2048, 4096], P(('grp', 'seq'), 'head'), parts along dimension 0, may hold values from -6 to 6
- values: bfloat16 [2048, 4096], P(('grp', 'seq'), 'head'), parts along dimension 0, may hold values from -6 to 6
- resid: bfloat16 [2048, 3072], P(('grp', 'seq'), 'head'), parts along dimension 0, may hold values from -6 to 6
- attn_gain: float32 [4096], P('head'), may hold values from 0.2 to 1.8
- out_weight: bfloat16 [4096, 3072], P('head', 'seq'), may hold values from -0.09375 to 0.09375
- moe_gain: float32 [3072], replicated, may hold values from 0.2 to 1.8
- routes: int32 [2048, 2], P(('grp', 'seq')), parts along dimension 0, may hold values from 0 to 7, all different within a row; in each aligned block of 128 rows (0 to 127, 128 to 255, ...) at most 36 rows name the same one
- route_weights: float32 [2048, 2], P(('grp', 'seq')), parts along dimension 0, may hold values from 0.2 to 1
- w_gate: bfloat16 [3072, 36864], P(None, ('seq', 'head')), may hold values from -0.109375 to 0.109375
- w_up: bfloat16 [3072, 36864], P(None, ('seq', 'head')), may hold values from -0.109375 to 0.109375
- w_down: bfloat16 [36864, 3072], P(('seq', 'head')), may hold values from -0.09375 to 0.09375
Outputs:
- mixed: bfloat16 [2048, 3072], P(('grp', 'seq'), 'head'), parts along dimension 0
The draws below stay inside these ranges and needn't reach their ends.
There are 2 independent parts, one for each index of `grp`. The reference program is written for one: setup_inputs(seed, part) draws one part's arguments, and reference() takes and returns one part's arrays. A program takes and returns all parts, laid end to end along the dimension named above; an argument that names none is the same for every part. Nothing has to cross between parts.
Inputs may be any that keep to these rules, and one draw needn't show every extreme that they name: A token's 2 experts differ. Within each aligned block of 128 tokens no expert is named by more than 36 routes, and in every draw some expert is named by exactly 36 routes of some block.
All inputs are finite; a program needn't handle non-finite values.
Results may differ from the reference program's by a relative error of at most 0.015.
Values may be sent and summed in bfloat16 or wider, within the bound.
A program may use at most 128 MiB of HBM per device.

```python
import math
import jax
import jax.numpy as jnp
import numpy as np
from jax import lax

D = 3072
HEADS = 32
HD = 128
EXPERTS = 8
FF = 4608
TOP = 2
TOK_DEV = 128
TOKENS = 1024
CAP = 36
SLICES = 2
FF_DEV = 2304


def steps_of(rng, shape, split, smallest, high):
    factor_of = 1.0
    for position, parts in split:
        draws = jax.random.uniform(jax.random.fold_in(jax.random.fold_in(rng, 6), position), (parts,), jnp.float32, smallest / len(split), high / len(split))
        factor_of = factor_of * jnp.repeat(jnp.exp(draws), shape[position] // parts).reshape((-1,) + (1,) * (len(shape) - 1 - position))
    return factor_of


def shared_out(key, own, number, rows, count, top, reach, skew):
    sequence = jax.random.permutation(key, count)
    crowded, ordinary = portions_of(count, rows * top, reach, skew, True), portions_of(count, rows * top, reach, skew, False)
    places = jnp.arange(count)

    def named(lengths, turn):
        used = int((lengths > 0).sum())
        fixed = max(1, used // 4)
        passed = fixed + (places - fixed + turn * (used - fixed)) % max(1, count - fixed)
        return jnp.zeros((count,), jnp.int32).at[sequence[jnp.where(places < fixed, places, passed)]].set(jnp.asarray(lengths, jnp.int32))

    lengths = jnp.where(number % 4 == 0, named(crowded, number // 4), named(ordinary, number - number // 4 - 1))
    mixed = jax.random.permutation(jax.random.fold_in(own, 3), count)
    donor, taker = mixed[0:count // 2 * 2:2], mixed[1:count // 2 * 2:2]
    slack = jnp.minimum(lengths[donor] - 1, reach - lengths[taker]) // 2
    slack = jnp.where((donor == sequence[0]) | (taker == sequence[0]) | (lengths[taker] == 0), 0, jnp.maximum(slack, 0))
    passed = jax.random.randint(jax.random.fold_in(own, 4), (count // 2,), 0, 1 << 20) % (slack + 1)
    lengths = lengths.at[donor].add(-passed).at[taker].add(passed)
    members = jnp.searchsorted(jnp.cumsum(lengths), jnp.arange(rows * top), side="right").astype(jnp.int32)
    table = members.reshape(top, rows).T
    table = table[jax.random.permutation(jax.random.fold_in(own, 1), rows)]
    turn = jax.random.randint(jax.random.fold_in(own, 2), (rows, 1), 0, top)
    return jnp.take_along_axis(table, (jnp.arange(top)[None, :] + turn) % top, axis=1)


def portions_of(amount, total, most, slope, full):
    portions = [(1 << 20) // math.isqrt(standing ** slope) + 1 for standing in range(1, amount + 1)]
    largest = most if full else min(most, max(-(-total // amount), total * portions[0] // sum(portions)))
    least = 1 if total - largest >= amount - 1 else 0
    holding, spare = [largest] + [least] * (amount - 1), total - largest - least * (amount - 1)
    while spare > 0:
        free = [i for i in range(1, amount) if holding[i] < largest] or [i for i in range(1, amount) if holding[i] < most]
        mass, left = sum([portions[i] for i in free]), spare
        for i in free:
            extra = min(most - holding[i], max(1, left * portions[i] // mass), spare)
            holding[i] = holding[i] + extra
            spare = spare - extra
    return np.array(holding)


def centred(key, extent, scale, bound, pieces=(), kind=jnp.bfloat16):
    drawn = scale * jax.random.normal(key, extent, jnp.float32)
    if pieces:
        drawn = drawn * steps_of(key, extent, pieces, -0.22, 0.18)
    return jnp.clip(drawn, -bound, bound).astype(kind)


def setup_inputs(seed: int = 0, part: int = 0) -> dict:
    streams_of = jax.random.split(jax.random.key(seed), 13)
    own_keys = jax.random.split(jax.random.fold_in(streams_of[12], part), 13)
    query = centred(own_keys[0], (TOKENS, HEADS * HD), 1.0, 6.0, ((0, 8), (1, 2)))
    keys = centred(own_keys[1], (TOKENS, HEADS * HD), 1.0, 6.0, ((0, 8), (1, 2)))
    values = centred(own_keys[2], (TOKENS, HEADS * HD), 1.0, 6.0, ((0, 8), (1, 2)))
    resid = centred(own_keys[3], (TOKENS, D), 1.0, 6.0, ((0, 8), (1, 2)))
    attn_gain = jnp.clip(1.0 + 0.16 * jax.random.normal(streams_of[4], (HEADS * HD,), jnp.float32), 0.2, 1.8)
    out_weight = centred(streams_of[5], (HEADS * HD, D), (HEADS * HD) ** -0.5, 0.09375, ((0, 2), (1, 8)))
    moe_gain = jnp.clip(1.0 + 0.16 * jax.random.normal(streams_of[6], (D,), jnp.float32), 0.2, 1.8)
    routes_keys = jax.random.split(jax.random.fold_in(own_keys[7], 1), TOKENS // TOK_DEV)
    routes_turns = jax.random.permutation(jax.random.fold_in(own_keys[7], 3), TOKENS // TOK_DEV)
    routes = jax.vmap(lambda own, number: shared_out(jax.random.fold_in(own_keys[7], 2), own, number, TOK_DEV, EXPERTS, TOP, CAP, 2))(routes_keys, routes_turns).reshape((TOKENS, TOP))
    route_weights = jnp.clip(0.2 + 0.8 * jax.random.uniform(own_keys[8], (TOKENS, TOP), jnp.float32) ** steps_of(own_keys[8], (TOKENS, TOP), ((0, 8),), -0.2, 0.2), 0.2, 1.0)
    w_gate = centred(streams_of[9], (D, EXPERTS * FF), D ** -0.5, 0.109375, ((1, 16),))
    w_up = centred(streams_of[10], (D, EXPERTS * FF), D ** -0.5, 0.109375, ((1, 16),))
    w_down = centred(streams_of[11], (EXPERTS * FF, D), FF ** -0.5, 0.09375, ((0, 16),))
    return dict(query=query, keys=keys, values=values, resid=resid, attn_gain=attn_gain, out_weight=out_weight, moe_gain=moe_gain, routes=routes, route_weights=route_weights, w_gate=w_gate, w_up=w_up, w_down=w_down)


EPS = 1e-06

def reference(query, keys, values, resid, attn_gain, out_weight, moe_gain, routes, route_weights, w_gate, w_up, w_down):
    blocks = TOKENS // TOK_DEV
    query_four_dims = query.astype(jnp.float32).reshape(blocks, TOK_DEV, HEADS, HD)
    k_four = keys.astype(jnp.float32).reshape(blocks, TOK_DEV, HEADS, HD)
    v_four = values.astype(jnp.float32).reshape(blocks, TOK_DEV, HEADS, HD)
    states = jnp.einsum('btnd,btne->bnde', k_four, v_four)
    running = jnp.cumsum(states, axis=0)
    earlier = jnp.concatenate([jnp.zeros_like(states[:1]), running[:-1]], axis=0)
    rounded_values = lax.optimization_barrier(earlier.astype(jnp.bfloat16)).astype(jnp.float32)
    inter = jnp.einsum('btnd,bnde->btne', query_four_dims, rounded_values)
    scores = jnp.einsum('btnd,bsnd->bnts', query_four_dims, k_four)
    causal = jnp.arange(TOK_DEV)[:, None] >= jnp.arange(TOK_DEV)[None, :]
    masked = lax.optimization_barrier(jnp.where(causal, scores, 0.0).astype(jnp.bfloat16)).astype(jnp.float32)
    inside_block_scores = jnp.einsum('bnts,bsne->btne', masked, v_four)
    attention = inter + inside_block_scores
    scale = lax.rsqrt(lax.optimization_barrier(jnp.mean(attention * attention, axis=-1, keepdims=True)) + EPS)
    normed = (attention * scale * attn_gain.reshape(HEADS, HD)).astype(jnp.bfloat16).reshape(TOKENS, HEADS * HD)
    projected = jnp.dot(normed, out_weight, preferred_element_type=jnp.float32)
    hidden = (resid.astype(jnp.float32) + projected).astype(jnp.bfloat16)
    wide = hidden.astype(jnp.float32)
    moe_in = (wide * lax.rsqrt(lax.optimization_barrier(jnp.mean(wide * wide, axis=-1, keepdims=True)) + EPS) * moe_gain).astype(jnp.bfloat16)
    block_routes = routes.reshape(blocks, TOK_DEV * TOP)
    expert_iota = jnp.arange(EXPERTS, dtype=jnp.int32)
    onehot = (block_routes[:, :, None] == expert_iota[None, None, :]).astype(jnp.int32)
    slots = lax.optimization_barrier(jnp.sum((jnp.cumsum(onehot, axis=1) - 1) * onehot, axis=2))
    block_ids = jnp.broadcast_to(jnp.arange(blocks, dtype=jnp.int32)[:, None], slots.shape)
    row_ids = (slots * blocks + block_ids).reshape(-1).astype(jnp.int32)
    expert_ids = routes.reshape(-1).astype(jnp.int32)
    token_ids = jnp.repeat(jnp.arange(TOKENS, dtype=jnp.int32), TOP)
    holding_arrays = jnp.zeros((EXPERTS, CAP * blocks, D), jnp.bfloat16).at[expert_ids, row_ids].set(moe_in[token_ids])
    gate_all = w_gate.reshape(D, EXPERTS, FF).transpose(1, 0, 2)
    up_all = w_up.reshape(D, EXPERTS, FF).transpose(1, 0, 2)
    down_all = w_down.reshape(EXPERTS, FF, D)

    def one_expert(operands):
        rows_in, gate_w, up_w, down_w = operands
        gate = jnp.dot(rows_in, gate_w, preferred_element_type=jnp.float32)
        upward = jnp.dot(rows_in, up_w, preferred_element_type=jnp.float32)
        inner = (jax.nn.silu(gate) * upward).astype(jnp.bfloat16)
        total = jnp.zeros((rows_in.shape[0], D), jnp.float32)
        for index in range(SLICES):
            part = jnp.dot(inner[:, index * FF_DEV:(index + 1) * FF_DEV], down_w[index * FF_DEV:(index + 1) * FF_DEV], preferred_element_type=jnp.float32)
            total = total + lax.optimization_barrier(part.astype(jnp.bfloat16)).astype(jnp.float32)
        return total
    expert_out = lax.map(one_expert, (holding_arrays, gate_all, up_all, down_all))
    picked = expert_out[expert_ids, row_ids].reshape(TOKENS, TOP, D)
    moe = lax.optimization_barrier(jnp.sum(picked * route_weights[:, :, None], axis=1))
    return (wide + moe).astype(jnp.bfloat16)
```

```python
import functools

import jax
import jax.numpy as jnp
from jax import lax
from jax.experimental import pallas as pl
from jax.experimental.pallas import tpu as pltpu
from jax.sharding import PartitionSpec as P

D = 3072
HD = 128
EXPERTS = 8
TOP = 2
CAP = 36


EPS = 1e-06
VMEM_MOST = 67043328


def swap_heads(x):
    pairs = [(i, lax.axis_size("head") - 1 - i) for i in range(lax.axis_size("head"))]
    return lax.ppermute(x, "head", pairs)


def greet_all(me, count, pair=False):
    barrier = pltpu.get_barrier_semaphore()

    def greet(step, carry):
        pl.semaphore_signal(
            barrier,
            inc=1,
            device_id={"seq": lax.rem(me + step, count)},
            device_id_type=pl.DeviceIdType.MESH,
        )
        return carry

    lax.fori_loop(1, count, greet, 0)
    if pair:
        pl.semaphore_signal(
            barrier,
            inc=1,
            device_id={"head": 1 - lax.axis_index("head")},
            device_id_type=pl.DeviceIdType.MESH,
        )
    pl.semaphore_wait(barrier, count - 1 + int(pair))


def grant(*blocks):
    total = 1 << 20
    for shape in blocks:
        cells = (-(-shape[-1] // 128) * 128) * (-(-shape[-2] // 16) * 16)
        for size in shape[:-2]:
            cells = cells * size
        total = total + 2 * cells
    return total


def send_to(src, dst, send_sem, recv_sem, **device):
    return pltpu.make_async_remote_copy(
        src_ref=src,
        dst_ref=dst,
        send_sem=send_sem,
        recv_sem=recv_sem,
        device_id=device,
        device_id_type=pl.DeviceIdType.MESH,
    )


def sums_kernel(count, own_ref, out_ref, got, made, send_sem, recv_sem, home_send, home_recv):
    me = lax.axis_index("seq")
    greet_all(me, count)

    def out(other):
        return send_to(
            own_ref.at[other], got.at[me], send_sem.at[other], recv_sem.at[me], seq=other
        )

    def arrival(other):
        return send_to(
            own_ref.at[other], got.at[other], send_sem.at[other], recv_sem.at[other], seq=other
        )

    def home(other):
        return send_to(
            made.at[other], out_ref.at[me], home_send.at[other], home_recv.at[me], seq=other
        )

    def home_arrival(other):
        return send_to(
            made.at[other], out_ref.at[other], home_send.at[other], home_recv.at[other], seq=other
        )

    def start(step, carry):
        out(lax.rem(me + step, count)).start()
        return carry

    lax.fori_loop(1, count, start, 0)
    got[me] = own_ref[me]

    def add(block, running):
        made[block] = running.astype(jnp.bfloat16)

        @pl.when(block != me)
        def _():
            arrival(block).wait_recv()
            home(block).start()

        return running + got[block].astype(jnp.float32)

    lax.fori_loop(0, count, add, jnp.zeros(got.shape[1:], jnp.float32))
    out_ref[me] = made[me]

    def finish(step, carry):
        other = lax.rem(me + step, count)
        out(other).wait_send()
        home_arrival(other).wait_recv()
        home(other).wait_send()
        return carry

    lax.fori_loop(1, count, finish, 0)


def earlier_sums(own):
    count = lax.axis_size("seq")
    shape = (count, own.shape[0] // count, own.shape[1])
    return pl.pallas_call(
        functools.partial(sums_kernel, count),
        name="sums",
        out_shape=jax.ShapeDtypeStruct(shape, jnp.bfloat16),
        in_specs=[pl.BlockSpec(memory_space=pltpu.VMEM)],
        out_specs=pl.BlockSpec(memory_space=pltpu.VMEM),
        scratch_shapes=[pltpu.VMEM(shape, jnp.bfloat16)] * 2
        + [pltpu.SemaphoreType.DMA((count,))] * 4,
        compiler_params=pltpu.CompilerParams(
            collective_id=1, has_side_effects=True, vmem_limit_bytes=grant(shape, shape, shape, shape, shape)
        ),
    )(own.reshape(shape)).reshape(own.shape)


def tile_of(size, most):
    fits = [n for n in range(128, min(size, most) + 1, 128) if size % n == 0]
    return max(fits) if fits else size


def experts_kernel(
    count,
    packed_ref,
    own_ref,
    high_ref,
    low_ref,
    gate_hbm,
    up_hbm,
    down_hbm,
    mixed_ref,
    rows,
    x,
    gate,
    up,
    inner,
    w_gate,
    w_up,
    w_down,
    mine,
    theirs,
    part,
    total,
    back,
    send_sem,
    recv_sem,
    pair_send,
    pair_recv,
    part_send,
    part_recv,
    home_send,
    home_recv,
    gate_sem,
    up_sem,
    down_sem,
    own_sem,
):
    me, head = lax.axis_index("seq"), lax.axis_index("head")
    cap, half = packed_ref.shape[1], packed_ref.shape[2]
    chunks, wide = rows.shape[1], rows.shape[4]
    hidden = inner.shape[1]
    tile = tile_of(hidden, 768)
    group = 4
    span = group * cap

    def start_row(side, chunk):
        return pl.multiple_of(jnp.where(side == 0, head, 1 - head) * half + chunk * wide, wide)

    def weights(side, chunk):
        ks = pl.ds(start_row(side, chunk), wide)
        spot = chunk * 2 + side
        return (
            pltpu.make_async_copy(gate_hbm.at[ks], w_gate.at[ks], gate_sem.at[spot]),
            pltpu.make_async_copy(up_hbm.at[ks], w_up.at[ks], up_sem.at[spot]),
        )

    down = pltpu.make_async_copy(down_hbm, w_down, down_sem)

    def fetch(spot, carry):
        for copy in weights(lax.rem(spot, 2), spot // 2):
            copy.start()
        return carry

    lax.fori_loop(0, 2 * chunks, fetch, 0)
    down.start()
    greet_all(me, count, True)

    def chunk_of(chunk):
        return pl.ds(pl.multiple_of(chunk * wide, wide), wide)

    def out(chunk, other):
        return send_to(
            packed_ref.at[other, :, chunk_of(chunk)],
            rows.at[0, chunk, me],
            send_sem.at[chunk, other],
            recv_sem.at[chunk, me],
            seq=other,
        )

    def arrival(chunk, other):
        return send_to(
            packed_ref.at[other, :, chunk_of(chunk)],
            rows.at[0, chunk, other],
            send_sem.at[chunk, other],
            recv_sem.at[chunk, other],
            seq=other,
        )

    def keep(chunk):
        return pltpu.make_async_copy(
            packed_ref.at[me, :, chunk_of(chunk)], rows.at[0, chunk, me], own_sem.at[chunk]
        )

    def pair(chunk):
        return send_to(
            rows.at[0, chunk], rows.at[1, chunk], pair_send.at[chunk], pair_recv.at[chunk], head=1 - head
        )

    def post(chunk, carry):
        def one(step, inside):
            out(chunk, lax.rem(me + step, count)).start()
            return inside

        lax.fori_loop(1, count, one, 0)
        keep(chunk).start()
        return carry

    lax.fori_loop(0, chunks, post, 0)
    gate[...] = jnp.zeros_like(gate)
    up[...] = jnp.zeros_like(up)

    def join(pages):
        return jnp.concatenate([page.astype(jnp.float32) for page in pages], axis=0).astype(jnp.bfloat16)

    def gather(side, chunk):
        def one(g, carry):
            x[pl.ds(pl.multiple_of(g * span, 16), span), :] = join(
                [rows[side, chunk, g * group + i] for i in range(group)]
            )
            return carry

        lax.fori_loop(0, count // group, one, 0)

    def accumulate(side, chunk):
        for copy in weights(side, chunk):
            copy.wait()
        gather(side, chunk)
        ks = pl.ds(start_row(side, chunk), wide)

        def one(n, carry):
            cols = pl.ds(pl.multiple_of(n * tile, tile), tile)
            gate[:, cols] += jnp.dot(x[...], w_gate[ks, cols], preferred_element_type=jnp.float32)
            up[:, cols] += jnp.dot(x[...], w_up[ks, cols], preferred_element_type=jnp.float32)
            return carry

        lax.fori_loop(0, hidden // tile, one, 0)

    def take(chunk, carry):
        def one(step, inside):
            arrival(chunk, lax.rem(me + count - step, count)).wait_recv()
            return inside

        lax.fori_loop(1, count, one, 0)
        keep(chunk).wait()
        pair(chunk).start()
        accumulate(0, chunk)
        pair(chunk).wait_recv()
        accumulate(1, chunk)
        return carry

    lax.fori_loop(0, chunks, take, 0)

    small = tile_of(hidden, 256)

    def activate(n, carry):
        cols = pl.ds(pl.multiple_of(n * small, small), small)
        inner[:, cols] = (jax.nn.silu(gate[:, cols]) * up[:, cols]).astype(jnp.bfloat16)
        return carry

    lax.fori_loop(0, hidden // small, activate, 0)
    down.wait()

    def hand(chunk):
        return send_to(mine.at[chunk], theirs.at[chunk], part_send.at[chunk], part_recv.at[chunk], head=1 - head)

    def home(chunk, other):
        return send_to(
            total.at[chunk, other],
            back.at[chunk, me],
            home_send.at[chunk, other],
            home_recv.at[chunk, me],
            seq=other,
        )

    def home_arrival(chunk, other):
        return send_to(
            total.at[chunk, other],
            back.at[chunk, other],
            home_send.at[chunk, other],
            home_recv.at[chunk, other],
            seq=other,
        )

    def project(side, chunk):
        cols = pl.ds(start_row(side, chunk), wide)
        part[...] = jnp.dot(inner[...], w_down[:, cols], preferred_element_type=jnp.float32)

    def give(chunk, carry):
        project(1, chunk)

        def split(g, inside):
            block = part[pl.ds(pl.multiple_of(g * span, 8), span), :]
            for i in range(group):
                mine[chunk, g * group + i] = block[i * cap : (i + 1) * cap].astype(jnp.bfloat16)
            return inside

        lax.fori_loop(0, count // group, split, 0)
        hand(chunk).start()
        project(0, chunk)
        hand(chunk).wait_recv()

        def add(g, inside):
            block = part[pl.ds(pl.multiple_of(g * span, 8), span), :]
            for i in range(group):
                spot = g * group + i
                total[chunk, spot] = (
                    block[i * cap : (i + 1) * cap] + theirs[chunk, spot].astype(jnp.float32)
                ).astype(jnp.bfloat16)
            return inside

        lax.fori_loop(0, count // group, add, 0)

        def one(step, inside):
            home(chunk, lax.rem(me + step, count)).start()
            return inside

        lax.fori_loop(1, count, one, 0)
        back[chunk, me] = total[chunk, me]
        return carry

    lax.fori_loop(0, chunks, give, 0)

    def mix(chunk, carry):
        def one(step, inside):
            home_arrival(chunk, lax.rem(me + count - step, count)).wait_recv()
            return inside

        lax.fori_loop(1, count, one, 0)

        def pack(g, inside):
            x[pl.ds(pl.multiple_of(g * span, 16), span), :] = join(
                [back[chunk, g * group + i] for i in range(group)]
            )
            return inside

        lax.fori_loop(0, count // group, pack, 0)
        cols = chunk_of(chunk)
        mixed_ref[:, cols] = (
            own_ref[:, cols].astype(jnp.float32)
            + jnp.dot(high_ref[...], x[...], preferred_element_type=jnp.float32)
            + jnp.dot(low_ref[...], x[...], preferred_element_type=jnp.float32)
        ).astype(jnp.bfloat16)
        return carry

    lax.fori_loop(0, chunks, mix, 0)

    def finish(chunk, carry):
        def one(step, inside):
            other = lax.rem(me + step, count)
            out(chunk, other).wait_send()
            home(chunk, other).wait_send()
            return inside

        lax.fori_loop(1, count, one, 0)
        pair(chunk).wait_send()
        hand(chunk).wait_send()
        return carry

    lax.fori_loop(0, chunks, finish, 0)


def experts(packed, own, high, low, w_gate, w_up, w_down):
    count, cap, half = packed.shape
    hidden = w_gate.shape[1]
    wide = tile_of(half, 512)
    chunks = half // wide
    rows = count * cap
    pages = (chunks, count, cap, wide)
    dma = pltpu.SemaphoreType.DMA
    vmem = pl.BlockSpec(memory_space=pltpu.VMEM)
    hbm = pl.BlockSpec(memory_space=pl.ANY)
    return pl.pallas_call(
        functools.partial(experts_kernel, count),
        name="experts",
        out_shape=jax.ShapeDtypeStruct(own.shape, jnp.bfloat16),
        in_specs=[vmem] * 4 + [hbm] * 3,
        out_specs=vmem,
        scratch_shapes=[
            pltpu.VMEM((2,) + pages, jnp.bfloat16),
            pltpu.VMEM((rows, wide), jnp.bfloat16),
            pltpu.VMEM((rows, hidden), jnp.float32),
            pltpu.VMEM((rows, hidden), jnp.float32),
            pltpu.VMEM((rows, hidden), jnp.bfloat16),
            pltpu.VMEM(w_gate.shape, jnp.bfloat16),
            pltpu.VMEM(w_up.shape, jnp.bfloat16),
            pltpu.VMEM(w_down.shape, jnp.bfloat16),
            pltpu.VMEM(pages, jnp.bfloat16),
            pltpu.VMEM(pages, jnp.bfloat16),
            pltpu.VMEM((rows, wide), jnp.float32),
            pltpu.VMEM(pages, jnp.bfloat16),
            pltpu.VMEM(pages, jnp.bfloat16),
            dma((chunks, count)),
            dma((chunks, count)),
            dma((chunks,)),
            dma((chunks,)),
            dma((chunks,)),
            dma((chunks,)),
            dma((chunks, count)),
            dma((chunks, count)),
            dma((2 * chunks,)),
            dma((2 * chunks,)),
            dma,
            dma((chunks,)),
        ],
        compiler_params=pltpu.CompilerParams(
            collective_id=2, has_side_effects=True, vmem_limit_bytes=VMEM_MOST
        ),
    )(packed, own, high, low, w_gate, w_up, w_down)


def project_kernel(
    count, shard_ref, weight_ref, back_ref, held, made, send_sem, recv_sem, back_send, back_recv, own_sem
):
    me = lax.axis_index("seq")
    outer, inner = me // 2, lax.rem(me, 2)
    outers = count // 2
    partner = outer * 2 + (1 - inner)
    greet_all(me, count)

    def pass_on(source, src, way, to):
        return pltpu.make_async_remote_copy(
            src_ref=src,
            dst_ref=held.at[source],
            send_sem=send_sem.at[source, way],
            recv_sem=recv_sem.at[source],
            device_id={"seq": to},
            device_id_type=pl.DeviceIdType.MESH,
        )

    def go_home(source):
        return pltpu.make_async_remote_copy(
            src_ref=made.at[source],
            dst_ref=back_ref.at[me],
            send_sem=back_send.at[source],
            recv_sem=back_recv.at[me],
            device_id={"seq": source},
            device_id_type=pl.DeviceIdType.MESH,
        )

    def multiply(source, block):
        made[source] = jnp.dot(
            block[...], weight_ref[...], preferred_element_type=jnp.float32
        ).astype(jnp.bfloat16)

    @pl.when(outer + 1 < outers)
    def _():
        pass_on(me, shard_ref, 0, me + 2).start()

    @pl.when(outer > 0)
    def _():
        pass_on(me, shard_ref, 1, me - 2).start()

    pass_on(me, shard_ref, 2, partner).start()
    multiply(me, shard_ref)
    own = pltpu.make_async_copy(made.at[me], back_ref.at[me], own_sem)
    own.start()

    def arrive(source):
        pass_on(source, held.at[source], 2, partner).wait_recv()

    def take(source):
        multiply(source, held.at[source])
        go_home(source).start()

    def step(distance, carry):
        low, high = me - 2 * distance, me + 2 * distance

        @pl.when(outer - distance >= 0)
        def _():
            arrive(low)

            @pl.when(outer + 1 < outers)
            def _():
                pass_on(low, held.at[low], 0, me + 2).start()

            pass_on(low, held.at[low], 2, partner).start()
            take(low)

        @pl.when(outer + distance < outers)
        def _():
            arrive(high)

            @pl.when(outer > 0)
            def _():
                pass_on(high, held.at[high], 1, me - 2).start()

            pass_on(high, held.at[high], 2, partner).start()
            take(high)

        for source in (
            jnp.where(outer - (distance - 1) >= 0, partner - 2 * (distance - 1), -1),
            jnp.where(
                (distance > 1) & (outer + (distance - 1) < outers), partner + 2 * (distance - 1), -1
            ),
        ):

            @pl.when(source >= 0)
            def _():
                arrive(source)
                take(source)

        return carry

    lax.fori_loop(1, outers + 1, step, 0)
    own.wait()

    def finish(step, carry):
        source = lax.rem(me + step, count)
        go_home(source).wait_send()
        pltpu.make_async_remote_copy(
            src_ref=made.at[source],
            dst_ref=back_ref.at[source],
            send_sem=back_send.at[source],
            recv_sem=back_recv.at[source],
            device_id={"seq": source},
            device_id_type=pl.DeviceIdType.MESH,
        ).wait_recv()
        return carry

    lax.fori_loop(1, count, finish, 0)

    def drain(step, carry):
        source = step * 2 + inner

        @pl.when((source <= me) & (outer + 1 < outers))
        def _():
            pass_on(source, held.at[source], 0, me + 2).wait_send()

        @pl.when((source >= me) & (outer > 0))
        def _():
            pass_on(source, held.at[source], 1, me - 2).wait_send()

        pass_on(source, held.at[source], 2, partner).wait_send()
        return carry

    lax.fori_loop(0, outers, drain, 0)


def project(normed, out_weight):
    count = lax.axis_size("seq")
    rows, width = normed.shape
    columns = out_weight.shape[1]
    return pl.pallas_call(
        functools.partial(project_kernel, count),
        name="project",
        out_shape=jax.ShapeDtypeStruct((count, rows, columns), jnp.bfloat16),
        in_specs=[pl.BlockSpec(memory_space=pltpu.VMEM)] * 2,
        out_specs=pl.BlockSpec(memory_space=pltpu.VMEM),
        scratch_shapes=[
            pltpu.VMEM((count, rows, width), jnp.bfloat16),
            pltpu.VMEM((count, rows, columns), jnp.bfloat16),
            pltpu.SemaphoreType.DMA((count, 3)),
            pltpu.SemaphoreType.DMA((count,)),
            pltpu.SemaphoreType.DMA((count,)),
            pltpu.SemaphoreType.DMA((count,)),
            pltpu.SemaphoreType.DMA,
        ],
        compiler_params=pltpu.CompilerParams(
            collective_id=0,
            has_side_effects=True,
            vmem_limit_bytes=grant(
                (count + 1, rows, width), (2 * count + 8, rows, columns), out_weight.shape
            ),
        ),
    )(normed, out_weight)


def per_device(
    query,
    keys,
    values,
    resid,
    attn_gain,
    out_weight,
    moe_gain,
    routes,
    route_weights,
    w_gate,
    w_up,
    w_down,
):
    tok_rows = query.shape[0]
    local_heads = query.shape[1] // HD
    seq_count = lax.axis_size("seq")
    head_count = lax.axis_size("head")
    head_pos = lax.axis_index("head")
    half_width = D // head_count
    slices = seq_count * head_count // EXPERTS
    q_three = query.reshape(tok_rows, local_heads, HD)
    k_three = keys.reshape(tok_rows, local_heads, HD)
    value_three_dims = values.reshape(tok_rows, local_heads, HD)
    block_own_state = jnp.einsum(
        "tnd,tne->nde", k_three, value_three_dims, preferred_element_type=jnp.float32
    )
    earlier = earlier_sums(
        block_own_state.astype(jnp.bfloat16).reshape(local_heads * HD, HD)
    ).reshape(local_heads, HD, HD)
    inter = jnp.einsum("tnd,nde->tne", q_three, earlier, preferred_element_type=jnp.float32)
    scores = jnp.einsum("tnd,snd->nts", q_three, k_three, preferred_element_type=jnp.float32)
    causal = jnp.arange(tok_rows)[:, None] >= jnp.arange(tok_rows)[None, :]
    resident_weight_parts = jnp.where(causal, scores, 0.0).astype(jnp.bfloat16)
    inside_block_scores = jnp.einsum(
        "rbj,jrh->brh", resident_weight_parts, value_three_dims, preferred_element_type=jnp.float32
    )
    attention = inter + inside_block_scores
    scale = lax.rsqrt(jnp.mean(attention * attention, axis=-1, keepdims=True) + EPS)
    normed = (
        (attention * scale * attn_gain.reshape(local_heads, HD))
        .astype(jnp.bfloat16)
        .reshape(tok_rows, local_heads * HD)
    )
    projected = (
        project(normed, out_weight).transpose(1, 0, 2).reshape(tok_rows, D).astype(jnp.float32)
    )
    placed = lax.dynamic_update_slice_in_dim(
        jnp.zeros((tok_rows, D), jnp.float32), resid.astype(jnp.float32), head_pos * half_width, 1
    )
    half = (projected + placed).astype(jnp.bfloat16)
    other = swap_heads(half)
    hidden = (half.astype(jnp.float32) + other.astype(jnp.float32)).astype(jnp.bfloat16)
    wide = hidden.astype(jnp.float32)
    moe_in = (
        wide * lax.rsqrt(jnp.mean(wide * wide, axis=-1, keepdims=True) + EPS) * moe_gain
    ).astype(jnp.bfloat16)
    own_rows = lax.dynamic_slice_in_dim(wide, head_pos * half_width, half_width, 1)
    flat_routes = routes.reshape(-1)
    onehot = (flat_routes[:, None] == jnp.arange(EXPERTS, dtype=jnp.int32)[None, :]).astype(
        jnp.int32
    )
    slots = jnp.sum((jnp.cumsum(onehot, axis=0) - 1) * onehot, axis=1)
    targets = (flat_routes * CAP + slots).reshape(tok_rows, TOP)
    slot_columns = jnp.arange(EXPERTS * CAP, dtype=jnp.int32)
    chosen = (targets[:, :, None] == slot_columns[None, None, :]).astype(jnp.float32)
    picker = jnp.sum(chosen, axis=1).astype(jnp.bfloat16)
    combine_weights = jnp.sum(chosen * route_weights[:, :, None], axis=1)
    contract_rows = (((0,), (0,)), ((), ()))
    own_half = lax.dynamic_slice_in_dim(moe_in, head_pos * half_width, half_width, 1)
    packed = lax.dot_general(
        picker, own_half, contract_rows, preferred_element_type=jnp.float32
    ).astype(jnp.bfloat16)
    chips = slices // head_count
    copies = jnp.broadcast_to(
        packed.reshape(EXPERTS, 1, CAP, half_width), (EXPERTS, chips, CAP, half_width)
    ).reshape(EXPERTS * chips, CAP, half_width)
    spread = jnp.broadcast_to(
        combine_weights.reshape(tok_rows, EXPERTS, 1, CAP), (tok_rows, EXPERTS, chips, CAP)
    ).reshape(tok_rows, EXPERTS * chips * CAP)
    high = spread.astype(jnp.bfloat16)
    low = (spread - high.astype(jnp.float32)).astype(jnp.bfloat16)
    return experts(copies, own_rows, high, low, w_gate, w_up, w_down)


def solution(mesh):
    return jax.shard_map(
        per_device,
        mesh=mesh,
        in_specs=(
            P(("grp", "seq"), "head"),
            P(("grp", "seq"), "head"),
            P(("grp", "seq"), "head"),
            P(("grp", "seq"), "head"),
            P("head"),
            P("head", "seq"),
            P(),
            P(("grp", "seq"), None),
            P(("grp", "seq"), None),
            P(None, ("seq", "head")),
            P(None, ("seq", "head")),
            P(("seq", "head"), None),
        ),
        out_specs=P(("grp", "seq"), "head"),
        check_vma=False,
    )
```

```python
import functools

import jax
import jax.numpy as jnp
from jax import lax
from jax.experimental import pallas as pl
from jax.experimental.pallas import tpu as pltpu
from jax.sharding import PartitionSpec as P

D = 3072
HD = 128
EXPERTS = 8
TOP = 2
CAP = 36


EPS = 1e-06
VMEM_MOST = 61 << 20
TOGETHER = 2


def greet_all(me, count, pair=False):
    barrier = pltpu.get_barrier_semaphore()

    def greet(step, carry):
        pl.semaphore_signal(
            barrier,
            inc=1,
            device_id={"seq": lax.rem(me + step, count)},
            device_id_type=pl.DeviceIdType.MESH,
        )
        return carry

    lax.fori_loop(1, count, greet, 0)
    if pair:
        pl.semaphore_signal(
            barrier,
            inc=1,
            device_id={"head": 1 - lax.axis_index("head")},
            device_id_type=pl.DeviceIdType.MESH,
        )
    pl.semaphore_wait(barrier, count - 1 + int(pair))


def send_to(src, dst, send_sem, recv_sem, **device):
    return pltpu.make_async_remote_copy(
        src_ref=src,
        dst_ref=dst,
        send_sem=send_sem,
        recv_sem=recv_sem,
        device_id=device,
        device_id_type=pl.DeviceIdType.MESH,
    )


def tile_of(size, most):
    fits = [n for n in range(128, min(size, most) + 1, 128) if size % n == 0]
    return max(fits) if fits else size


def experts_kernel(
    count,
    packed_ref,
    own_ref,
    high_ref,
    low_ref,
    gate_hbm,
    up_hbm,
    down_hbm,
    mixed_ref,
    rows,
    x,
    gate,
    up,
    inner,
    w_gate,
    w_up,
    w_down,
    mine,
    theirs,
    part,
    total,
    back,
    send_sem,
    recv_sem,
    pair_send,
    pair_recv,
    part_send,
    part_recv,
    home_send,
    home_recv,
    gate_sem,
    up_sem,
    down_sem,
    own_sem,
):
    me, head = lax.axis_index("seq"), lax.axis_index("head")
    cap, half = packed_ref.shape[1], packed_ref.shape[2]
    chips = count // packed_ref.shape[0]
    chunks, wide = rows.shape[1], rows.shape[4]
    hidden = inner.shape[1]
    tile = tile_of(hidden, 768)
    group = 4
    span = group * cap

    def start_row(side, chunk):
        return pl.multiple_of(jnp.where(side == 0, head, 1 - head) * half + chunk * wide, wide)

    def weights(side, chunk):
        ks = pl.ds(start_row(side, chunk), wide)
        spot = chunk * 2 + side
        return (
            pltpu.make_async_copy(gate_hbm.at[ks], w_gate.at[ks], gate_sem.at[spot]),
            pltpu.make_async_copy(up_hbm.at[ks], w_up.at[ks], up_sem.at[spot]),
        )

    down = pltpu.make_async_copy(down_hbm, w_down, down_sem)

    def fetch(spot, carry):
        for copy in weights(lax.rem(spot, 2), spot // 2):
            copy.start()
        return carry

    lax.fori_loop(0, 2 * chunks, fetch, 0)
    down.start()
    greet_all(me, count, True)

    def chunk_of(chunk):
        return pl.ds(pl.multiple_of(chunk * wide, wide), wide)

    def out(chunk, other):
        return send_to(
            packed_ref.at[other // chips, :, chunk_of(chunk)],
            rows.at[0, chunk, me],
            send_sem.at[chunk, other],
            recv_sem.at[chunk, me],
            seq=other,
        )

    def arrival(chunk, other):
        return send_to(
            packed_ref.at[other // chips, :, chunk_of(chunk)],
            rows.at[0, chunk, other],
            send_sem.at[chunk, other],
            recv_sem.at[chunk, other],
            seq=other,
        )

    def keep(chunk):
        return pltpu.make_async_copy(
            packed_ref.at[me // chips, :, chunk_of(chunk)], rows.at[0, chunk, me], own_sem.at[chunk]
        )

    def pair(chunk):
        return send_to(
            rows.at[0, chunk], rows.at[1, chunk], pair_send.at[chunk], pair_recv.at[chunk], head=1 - head
        )

    def post(chunk, carry):
        def one(step, inside):
            out(chunk, lax.rem(me + step, count)).start()
            return inside

        lax.fori_loop(1, count, one, 0)
        keep(chunk).start()
        return carry

    lax.fori_loop(0, chunks, post, 0)
    gate[...] = jnp.zeros_like(gate)
    up[...] = jnp.zeros_like(up)

    def join(pages):
        return jnp.concatenate([page.astype(jnp.float32) for page in pages], axis=0).astype(jnp.bfloat16)

    def gather(side, chunk):
        def one(g, carry):
            x[pl.ds(pl.multiple_of(g * span, 16), span), :] = join(
                [rows[side, chunk, g * group + i] for i in range(group)]
            )
            return carry

        lax.fori_loop(0, count // group, one, 0)

    def accumulate(side, chunk):
        for copy in weights(side, chunk):
            copy.wait()
        gather(side, chunk)
        ks = pl.ds(start_row(side, chunk), wide)

        def one(n, carry):
            cols = pl.ds(pl.multiple_of(n * tile, tile), tile)
            gate[:, cols] += jnp.dot(x[...], w_gate[ks, cols], preferred_element_type=jnp.float32)
            up[:, cols] += jnp.dot(x[...], w_up[ks, cols], preferred_element_type=jnp.float32)
            return carry

        lax.fori_loop(0, hidden // tile, one, 0)

    def take(chunk, carry):
        def one(step, inside):
            arrival(chunk, lax.rem(me + count - step, count)).wait_recv()
            return inside

        lax.fori_loop(1, count, one, 0)
        keep(chunk).wait()
        pair(chunk).start()
        accumulate(0, chunk)
        pair(chunk).wait_recv()
        accumulate(1, chunk)
        return carry

    lax.fori_loop(0, chunks, take, 0)

    small = tile_of(hidden, 256)

    def activate(n, carry):
        cols = pl.ds(pl.multiple_of(n * small, small), small)
        inner[:, cols] = (jax.nn.silu(gate[:, cols]) * up[:, cols]).astype(jnp.bfloat16)
        return carry

    lax.fori_loop(0, hidden // small, activate, 0)
    down.wait()

    def hand(chunk):
        return send_to(mine.at[chunk], theirs.at[chunk], part_send.at[chunk], part_recv.at[chunk], head=1 - head)

    def home(chunk, other):
        return send_to(
            total.at[chunk, other],
            back.at[chunk, me],
            home_send.at[chunk, other],
            home_recv.at[chunk, me],
            seq=other,
        )

    def home_arrival(chunk, other):
        return send_to(
            total.at[chunk, other],
            back.at[chunk, other],
            home_send.at[chunk, other],
            home_recv.at[chunk, other],
            seq=other,
        )

    def project(side, chunk):
        cols = pl.ds(start_row(side, chunk), wide)
        part[...] = jnp.dot(inner[...], w_down[:, cols], preferred_element_type=jnp.float32)

    def give(chunk, carry):
        project(1, chunk)

        def split(g, inside):
            block = part[pl.ds(pl.multiple_of(g * span, 8), span), :]
            for i in range(group):
                mine[chunk, g * group + i] = block[i * cap : (i + 1) * cap].astype(jnp.bfloat16)
            return inside

        lax.fori_loop(0, count // group, split, 0)
        hand(chunk).start()
        project(0, chunk)
        hand(chunk).wait_recv()

        def add(g, inside):
            block = part[pl.ds(pl.multiple_of(g * span, 8), span), :]
            for i in range(group):
                spot = g * group + i
                total[chunk, spot] = (
                    block[i * cap : (i + 1) * cap] + theirs[chunk, spot].astype(jnp.float32)
                ).astype(jnp.bfloat16)
            return inside

        lax.fori_loop(0, count // group, add, 0)

        def one(step, inside):
            home(chunk, lax.rem(me + step, count)).start()
            return inside

        lax.fori_loop(1, count, one, 0)
        back[chunk, me] = total[chunk, me]
        return carry

    lax.fori_loop(0, chunks, give, 0)

    rows_of = (((0,), (0,)), ((), ()))

    def mix(chunk, carry):
        def one(step, inside):
            home_arrival(chunk, lax.rem(me + count - step, count)).wait_recv()
            return inside

        lax.fori_loop(1, count, one, 0)

        def pack(g, inside):
            x[pl.ds(pl.multiple_of(g * span, 16), span), :] = join(
                [back[chunk, g * group + i] for i in range(group)]
            )
            return inside

        lax.fori_loop(0, count // group, pack, 0)
        cols = chunk_of(chunk)
        mixed_ref[:, cols] = (
            own_ref[:, cols].astype(jnp.float32)
            + lax.dot_general(high_ref[...], x[...], rows_of, preferred_element_type=jnp.float32)
            + lax.dot_general(low_ref[...], x[...], rows_of, preferred_element_type=jnp.float32)
        ).astype(jnp.bfloat16)
        return carry

    lax.fori_loop(0, chunks, mix, 0)

    def finish(chunk, carry):
        def one(step, inside):
            other = lax.rem(me + step, count)
            out(chunk, other).wait_send()
            home(chunk, other).wait_send()
            return inside

        lax.fori_loop(1, count, one, 0)
        pair(chunk).wait_send()
        hand(chunk).wait_send()
        return carry

    lax.fori_loop(0, chunks, finish, 0)


def experts(packed, own, high, low, w_gate, w_up, w_down):
    count = lax.axis_size("seq")
    _, cap, half = packed.shape
    hidden = w_gate.shape[1]
    wide = tile_of(half, 512)
    chunks = half // wide
    rows = count * cap
    pages = (chunks, count, cap, wide)
    dma = pltpu.SemaphoreType.DMA
    vmem = pl.BlockSpec(memory_space=pltpu.VMEM)
    hbm = pl.BlockSpec(memory_space=pltpu.HBM)
    return pl.pallas_call(
        functools.partial(experts_kernel, count),
        name="experts",
        out_shape=jax.ShapeDtypeStruct(own.shape, jnp.bfloat16),
        in_specs=[vmem] * 4 + [hbm] * 3,
        out_specs=vmem,
        scratch_shapes=[
            pltpu.VMEM((2,) + pages, jnp.bfloat16),
            pltpu.VMEM((rows, wide), jnp.bfloat16),
            pltpu.VMEM((rows, hidden), jnp.float32),
            pltpu.VMEM((rows, hidden), jnp.float32),
            pltpu.VMEM((rows, hidden), jnp.bfloat16),
            pltpu.VMEM(w_gate.shape, jnp.bfloat16),
            pltpu.VMEM(w_up.shape, jnp.bfloat16),
            pltpu.VMEM(w_down.shape, jnp.bfloat16),
            pltpu.VMEM(pages, jnp.bfloat16),
            pltpu.VMEM(pages, jnp.bfloat16),
            pltpu.VMEM((rows, wide), jnp.float32),
            pltpu.VMEM(pages, jnp.bfloat16),
            pltpu.VMEM(pages, jnp.bfloat16),
            dma((chunks, count)),
            dma((chunks, count)),
            dma((chunks,)),
            dma((chunks,)),
            dma((chunks,)),
            dma((chunks,)),
            dma((chunks, count)),
            dma((chunks, count)),
            dma((2 * chunks,)),
            dma((2 * chunks,)),
            dma,
            dma((chunks,)),
        ],
        compiler_params=pltpu.CompilerParams(
            collective_id=2, has_side_effects=True, vmem_limit_bytes=VMEM_MOST
        ),
    )(packed, own, high, low, w_gate, w_up, w_down)


def mixer_kernel(
    count,
    query_hbm,
    keys_hbm,
    values_hbm,
    weight_hbm,
    resid_hbm,
    head_gain_ref,
    gain_ref,
    routes_ref,
    route_weights_ref,
    packed_ref,
    own_ref,
    high_ref,
    low_ref,
    query,
    keys,
    values,
    resid,
    weight,
    swap_give,
    swap_got,
    own_state,
    chain_got,
    chain_give,
    first_give,
    first_got,
    before,
    inside,
    normed,
    held,
    give,
    got,
    acc,
    cross_give,
    cross_got,
    home_give,
    home,
    square_give,
    square_got,
    load_sem,
    swap_send,
    swap_recv,
    chain_send,
    chain_recv,
    first_send,
    first_recv,
    w_send,
    w_recv,
    a_send,
    a_recv,
    pass_send,
    give_send,
    give_recv,
    cross_send,
    cross_recv,
    home_send,
    home_recv,
    square_send,
    square_recv,
):
    me, head = lax.axis_index("seq"), lax.axis_index("head")
    outer, inner = me // 2, lax.rem(me, 2)
    outers = count // 2
    partner = outer * 2 + (1 - inner)
    rows, width = query.shape
    quarter = width // 2
    heads = quarter // HD
    groups, together = swap_give.shape[0], swap_give.shape[1]
    same = head == inner
    cross = jnp.logical_not(same)
    kept = outers // 2
    target_head = outer // kept
    f32, bf16 = jnp.float32, jnp.bfloat16

    loads = [
        pltpu.make_async_copy(src, dst, load_sem.at[i])
        for i, (src, dst) in enumerate(
            ((keys_hbm, keys), (values_hbm, values), (query_hbm, query), (resid_hbm, resid))
        )
    ]
    for load in loads:
        load.start()

    barrier = pltpu.get_barrier_semaphore()

    def greet(**device):
        pl.semaphore_signal(barrier, inc=1, device_id=device, device_id_type=pl.DeviceIdType.MESH)

    def greet_column(step, carry):
        other = lax.rem(outer + step, outers) * 2 + inner
        greet(seq=other)
        greet(seq=other, head=1 - head)
        return carry

    lax.fori_loop(1, outers, greet_column, 0)
    greet(head=1 - head)
    greet(seq=partner)
    greet(seq=partner, head=1 - head)

    def lanes_of(n):
        return pl.ds(pl.multiple_of(n * HD, HD), HD)

    def state(n):
        return lax.dot_general(
            keys[:, lanes_of(n)],
            values[:, lanes_of(n)],
            (((0,), (0,)), ((), ())),
            preferred_element_type=f32,
        )

    loads[0].wait()
    loads[1].wait()

    def other_states(g, carry):
        for i in range(together):
            swap_give[g, i] = state((1 - inner) * heads + g * together + i).astype(bf16)
        return carry

    lax.fori_loop(0, groups, other_states, 0)
    pl.semaphore_wait(barrier, 2 * outers + 1)

    def swap(g):
        return send_to(swap_give.at[g], swap_got.at[g], swap_send.at[g], swap_recv.at[g], seq=partner)

    def chain(g):
        return send_to(chain_give.at[g], chain_got.at[g], chain_send.at[g], chain_recv.at[g], seq=me + 2)

    def first(g):
        return send_to(first_give.at[g], first_got.at[g], first_send.at[g], first_recv.at[g], seq=partner)

    def post(g, carry):
        swap(g).start()
        return carry

    lax.fori_loop(0, groups, post, 0)

    def cut(which):
        return pl.ds(pl.multiple_of(which * quarter, quarter), quarter)

    w_local = pltpu.make_async_copy(weight_hbm.at[cut(head)], weight.at[inner], w_recv.at[0])
    w_near = send_to(
        weight_hbm.at[cut(1 - head)], weight.at[inner], w_send.at[1], w_recv.at[0], head=1 - head
    )
    w_straight = send_to(
        weight_hbm.at[cut(head)], weight.at[inner], w_send.at[0], w_recv.at[1], seq=partner
    )
    w_turned = send_to(
        weight_hbm.at[cut(1 - head)],
        weight.at[inner],
        w_send.at[1],
        w_recv.at[1],
        seq=partner,
        head=1 - head,
    )

    @pl.when(same)
    def _():
        w_local.start()
        w_near.start()

    def own_states(g, carry):
        for i in range(together):
            own_state[g, i] = state(inner * heads + g * together + i)
        return carry

    lax.fori_loop(0, groups, own_states, 0)
    loads[2].wait()
    token = lax.broadcasted_iota(jnp.int32, (rows, rows), 0)
    causal = token >= lax.broadcasted_iota(jnp.int32, (rows, rows), 1)

    def within(n):
        scores = lax.dot_general(
            query[:, lanes_of(n)],
            keys[:, lanes_of(n)],
            (((1,), (1,)), ((), ())),
            preferred_element_type=f32,
        )
        masked = jnp.where(causal, scores, 0.0).astype(bf16)
        inside[n] = jnp.dot(masked, values[:, lanes_of(n)], preferred_element_type=f32)

    def link(g, carry):
        swap(g).wait_recv()

        @pl.when(outer > 0)
        def _():
            chain(g).wait_recv()

        start = jnp.where(outer > 0, chain_got[g].astype(f32), 0.0)
        mine, theirs = own_state[g], swap_got[g].astype(f32)
        chain_give[g] = (start + mine + theirs).astype(bf16)
        first_give[g] = (start + jnp.where(inner == 0, mine, 0.0)).astype(bf16)
        before[g] = (start + jnp.where(inner == 1, theirs, 0.0)).astype(bf16)

        @pl.when(outer + 1 < outers)
        def _():
            chain(g).start()

        first(g).start()
        for i in range(2 * together):
            within(g * 2 * together + i)
        return carry

    @pl.when(outer == 0)
    def _():
        chain_got[...] = jnp.zeros_like(chain_got)

    lax.fori_loop(0, groups, link, 0)

    def attend(n, prefix):
        attention = inside[n] + jnp.dot(query[:, lanes_of(n)], prefix, preferred_element_type=f32)
        scale = lax.rsqrt(jnp.mean(attention * attention, axis=-1, keepdims=True) + EPS)
        normed[:, lanes_of(n)] = (attention * scale * head_gain_ref[:, lanes_of(n)]).astype(bf16)

    def attend_first(g, carry):
        for i in range(together):
            attend(inner * heads + g * together + i, before[g, i])
        return carry

    lax.fori_loop(0, groups, attend_first, 0)

    def a_remote(which, recv, **device):
        return send_to(
            normed.at[:, cut(which)], held.at[outer, inner], a_send.at[0], a_recv.at[outer, inner], **device
        )

    a_local = pltpu.make_async_copy(
        normed.at[:, cut(inner)], held.at[outer, inner], a_recv.at[outer, inner]
    )
    a_turned = a_remote(inner, 1, seq=partner, head=1 - head)
    a_near = send_to(
        normed.at[:, cut(1 - inner)],
        held.at[outer, inner],
        a_send.at[1],
        a_recv.at[outer, inner],
        head=1 - head,
    )
    a_straight = send_to(
        normed.at[:, cut(1 - inner)],
        held.at[outer, inner],
        a_send.at[1],
        a_recv.at[outer, inner],
        seq=partner,
    )

    @pl.when(same)
    def _():
        a_local.start()

    @pl.when(cross)
    def _():
        a_turned.start()

    def attend_second(g, carry):
        first(g).wait_recv()
        for i in range(together):
            attend((1 - inner) * heads + g * together + i, first_got[g, i])
        return carry

    lax.fori_loop(0, groups, attend_second, 0)

    @pl.when(same)
    def _():
        a_near.start()

    @pl.when(cross)
    def _():
        a_straight.start()
        w_straight.start()
        w_turned.start()

    experts_count, cap = packed_ref.shape[0], packed_ref.shape[1]
    places = high_ref.shape[0]
    chips = count // experts_count
    expert = lax.broadcasted_iota(jnp.int32, (16, rows), 0)
    names = [routes_ref[j : j + 1, :] for j in range(TOP)]
    marks = sum((expert == name).astype(f32) for name in names)
    later = (token < lax.broadcasted_iota(jnp.int32, (rows, rows), 1)).astype(bf16)
    ahead = jnp.dot(marks.astype(bf16), later, preferred_element_type=f32)
    slots = [
        jnp.sum(jnp.where(expert == name, ahead, 0.0), axis=0, keepdims=True).astype(jnp.int32)
        for name in names
    ]
    place = lax.broadcasted_iota(jnp.int32, (places, rows), 0)
    factors = jnp.zeros((places, rows), f32)
    for j in range(TOP):
        for chip in range(chips):
            hit = place == (names[j] * chips + chip) * cap + slots[j]
            factors = factors + jnp.where(hit, route_weights_ref[j : j + 1, :], 0.0)
    high = factors.astype(bf16)
    high_ref[...] = high
    low_ref[...] = (factors - high.astype(f32)).astype(bf16)

    def move(source, side, up):
        return send_to(
            held.at[source, side],
            held.at[source, side],
            pass_send.at[source, side, up],
            a_recv.at[source, side],
            seq=me + (2 if up else -2),
        )

    def forward(source, side):
        @pl.when((source <= outer) & (outer + 1 < outers))
        def _():
            move(source, side, 1).start()

        @pl.when((source >= outer) & (outer > 0))
        def _():
            move(source, side, 0).start()

    def arrive(source):
        for turn in range(2):
            side = head if turn == 0 else 1 - head
            move(source, side, 0).wait_recv()
            forward(source, side)

    def own_near():
        @pl.when(same)
        def _():
            a_local.wait()

        @pl.when(cross)
        def _():
            a_near.wait_recv()

        forward(outer, inner)

    def own_far():
        send_to(
            normed.at[:, cut(0)], held.at[outer, 1 - inner], a_send.at[0], a_recv.at[outer, 1 - inner], seq=partner
        ).wait_recv()
        forward(outer, 1 - inner)

    @pl.when(same)
    def _():
        own_near()
        own_far()

    @pl.when(cross)
    def _():
        own_far()
        own_near()

    def hand(source):
        return send_to(give.at[source], got.at[source], give_send.at[source], give_recv.at[source], head=1 - head)

    def over(source):
        return send_to(
            cross_give.at[source], cross_got.at[source], cross_send.at[source], cross_recv.at[source], seq=partner
        )

    spot = lax.rem(outer, kept) * 2 + head

    def home_to(source):
        return send_to(
            home_give.at[source],
            home.at[spot],
            home_send.at[source],
            home_recv.at[spot],
            seq=source * 2 + inner,
            head=target_head,
        )

    home_own = pltpu.make_async_copy(home_give.at[outer], home.at[spot], home_recv.at[spot])
    stays = head == target_head

    def multiply(source):
        block = held[source].reshape(2 * rows, quarter)
        give[source] = (
            jnp.dot(block, weight[1 - head], preferred_element_type=f32)
            .astype(bf16)
            .reshape(give.shape[1:])
        )
        hand(source).start()
        acc[source] = jnp.dot(block, weight[head], preferred_element_type=f32).reshape(acc.shape[1:])

    def reduce_pair(source):
        hand(source).wait_recv()
        cross_give[source] = (
            acc[source, 1 - inner] + got[source, 1 - inner].astype(f32)
        ).astype(bf16)
        over(source).start()
        acc[source, inner] = acc[source, inner] + got[source, inner].astype(f32)

    def send_home(source):
        over(source).wait_recv()
        home_give[source] = (acc[source, inner] + cross_got[source].astype(f32)).astype(bf16)

        @pl.when((source == outer) & stays)
        def _():
            home_own.start()

        @pl.when(jnp.logical_not((source == outer) & stays))
        def _():
            home_to(source).start()

    def near(distance, action):
        @pl.when((outer - distance >= 0) & (distance > 0))
        def _():
            action(outer - distance)

        @pl.when(outer + distance < outers)
        def _():
            action(outer + distance)

    near(1, arrive)

    @pl.when(same)
    def _():
        w_local.wait()

    @pl.when(cross)
    def _():
        w_near.wait_recv()

    send_to(
        weight_hbm.at[cut(0)], weight.at[1 - inner], w_send.at[0], w_recv.at[1], seq=partner
    ).wait_recv()
    multiply(outer)
    near(1, multiply)
    reduce_pair(outer)
    near(1, reduce_pair)
    send_home(outer)

    def step(distance, carry):
        near(distance, arrive)
        near(distance, multiply)
        near(distance - 1, send_home)
        near(distance, reduce_pair)
        return carry

    lax.fori_loop(2, outers, step, 0)
    near(outers - 1, send_home)

    def collect(piece, carry):
        source = head * kept + piece // 2
        local = (source == outer) & (lax.rem(piece, 2) == head)

        @pl.when(local)
        def _():
            home_own.wait()

        @pl.when(jnp.logical_not(local))
        def _():
            send_to(
                home_give.at[0], home.at[piece], home_send.at[0], home_recv.at[piece], head=1 - head
            ).wait_recv()

        return carry

    lax.fori_loop(0, 2 * kept, collect, 0)
    loads[3].wait()
    projected = jnp.concatenate([home[piece].astype(f32) for piece in range(2 * kept)], axis=1)
    hidden = (projected + resid[...].astype(f32)).astype(bf16)
    own_ref[...] = hidden
    wide = hidden.astype(f32)
    square = jnp.sum(wide * wide, axis=1, keepdims=True)
    square_give[...] = jnp.broadcast_to(square, square_give.shape)
    trade = send_to(square_give, square_got, square_send, square_recv, head=1 - head)
    trade.start()
    pick = lax.broadcasted_iota(jnp.int32, (experts_count * cap, rows), 0)
    picker = sum((pick == names[j] * cap + slots[j]).astype(f32) for j in range(TOP)).astype(bf16)
    trade.wait_recv()
    half = resid.shape[1]
    scale = lax.rsqrt((square + square_got[:, 0:1]) / (2 * half) + EPS)
    gain = gain_ref[:, pl.ds(pl.multiple_of(head * half, half), half)]
    moe_in = (wide * scale * gain).astype(bf16)
    chosen = jnp.dot(picker, moe_in, preferred_element_type=f32)
    for page in range(experts_count):
        packed_ref[page] = chosen[page * cap : (page + 1) * cap].astype(bf16)

    trade.wait_send()

    @pl.when(same)
    def _():
        w_near.wait_send()
        a_near.wait_send()

    @pl.when(cross)
    def _():
        w_straight.wait_send()
        w_turned.wait_send()
        a_turned.wait_send()
        a_straight.wait_send()

    def finish_group(g, carry):
        swap(g).wait_send()
        first(g).wait_send()

        @pl.when(outer + 1 < outers)
        def _():
            chain(g).wait_send()

        return carry

    lax.fori_loop(0, groups, finish_group, 0)

    def finish(source, carry):
        hand(source).wait_send()
        over(source).wait_send()

        @pl.when(jnp.logical_not((source == outer) & stays))
        def _():
            home_to(source).wait_send()

        for side in range(2):

            @pl.when((source <= outer) & (outer + 1 < outers))
            def _():
                move(source, side, 1).wait_send()

            @pl.when((source >= outer) & (outer > 0))
            def _():
                move(source, side, 0).wait_send()

        return carry

    lax.fori_loop(0, outers, finish, 0)


def mixer(query, keys, values, out_weight, resid, attn_gain, moe_gain, routes, route_weights):
    count = lax.axis_size("seq")
    outers = count // 2
    rows, width = query.shape
    columns = out_weight.shape[1]
    half = resid.shape[1]
    heads = width // HD // 2
    together = TOGETHER
    groups = heads // together
    dma = pltpu.SemaphoreType.DMA
    vmem = pl.BlockSpec(memory_space=pltpu.VMEM)
    hbm = pl.BlockSpec(memory_space=pltpu.HBM)
    bf16, f32 = jnp.bfloat16, jnp.float32
    states = (groups, together, HD, HD)
    return pl.pallas_call(
        functools.partial(mixer_kernel, count),
        name="mixer",
        out_shape=(
            jax.ShapeDtypeStruct((EXPERTS, CAP, half), bf16),
            jax.ShapeDtypeStruct((rows, half), bf16),
            jax.ShapeDtypeStruct((count * CAP, rows), bf16),
            jax.ShapeDtypeStruct((count * CAP, rows), bf16),
        ),
        in_specs=[hbm] * 5 + [vmem] * 4,
        out_specs=(vmem,) * 4,
        scratch_shapes=[
            pltpu.VMEM((rows, width), bf16),
            pltpu.VMEM((rows, width), bf16),
            pltpu.VMEM((rows, width), bf16),
            pltpu.VMEM((rows, half), bf16),
            pltpu.VMEM((2, width // 2, columns), bf16),
            pltpu.VMEM(states, bf16),
            pltpu.VMEM(states, bf16),
            pltpu.VMEM(states, f32),
            pltpu.VMEM(states, bf16),
            pltpu.VMEM(states, bf16),
            pltpu.VMEM(states, bf16),
            pltpu.VMEM(states, bf16),
            pltpu.VMEM(states, bf16),
            pltpu.VMEM((2 * heads, rows, HD), f32),
            pltpu.VMEM((rows, width), bf16),
            pltpu.VMEM((outers, 2, rows, width // 2), bf16),
            pltpu.VMEM((outers, 2, rows, columns), bf16),
            pltpu.VMEM((outers, 2, rows, columns), bf16),
            pltpu.VMEM((outers, 2, rows, columns), f32),
            pltpu.VMEM((outers, rows, columns), bf16),
            pltpu.VMEM((outers, rows, columns), bf16),
            pltpu.VMEM((outers, rows, columns), bf16),
            pltpu.VMEM((outers, rows, columns), bf16),
            pltpu.VMEM((rows, 128), f32),
            pltpu.VMEM((rows, 128), f32),
            dma((4,)),
            dma((groups,)),
            dma((groups,)),
            dma((groups,)),
            dma((groups,)),
            dma((groups,)),
            dma((groups,)),
            dma((2,)),
            dma((2,)),
            dma((2,)),
            dma((outers, 2)),
            dma((outers, 2, 2)),
            dma((outers,)),
            dma((outers,)),
            dma((outers,)),
            dma((outers,)),
            dma((outers,)),
            dma((outers,)),
            dma,
            dma,
        ],
        compiler_params=pltpu.CompilerParams(
            collective_id=0, has_side_effects=True, vmem_limit_bytes=63 << 20
        ),
    )(
        query,
        keys,
        values,
        out_weight,
        resid,
        attn_gain.reshape(1, width),
        moe_gain.reshape(1, 2 * half),
        routes.T,
        route_weights.T,
    )


def per_device(
    query,
    keys,
    values,
    resid,
    attn_gain,
    out_weight,
    moe_gain,
    routes,
    route_weights,
    w_gate,
    w_up,
    w_down,
):
    packed, own, high, low = mixer(
        query, keys, values, out_weight, resid, attn_gain, moe_gain, routes, route_weights
    )
    return experts(packed, own, high, low, w_gate, w_up, w_down)


def solution(mesh):
    return jax.shard_map(
        per_device,
        mesh=mesh,
        in_specs=(
            P(("grp", "seq"), "head"),
            P(("grp", "seq"), "head"),
            P(("grp", "seq"), "head"),
            P(("grp", "seq"), "head"),
            P("head"),
            P("head", "seq"),
            P(),
            P(("grp", "seq"), None),
            P(("grp", "seq"), None),
            P(None, ("seq", "head")),
            P(None, ("seq", "head")),
            P(("seq", "head"), None),
        ),
        out_specs=P(("grp", "seq"), "head"),
        check_vma=False,
    )
```

```python
import functools

import jax
import jax.numpy as jnp
from jax import lax
from jax.experimental import pallas as pl
from jax.experimental.pallas import tpu as pltpu
from jax.sharding import PartitionSpec as P

D = 3072
HD = 128
EXPERTS = 8
TOP = 2
CAP = 36


EPS = 1e-06
VMEM_MOST = 67043328
TOGETHER = 2


def send_to(src, dst, send_sem, recv_sem, **device):
    return pltpu.make_async_remote_copy(
        src_ref=src,
        dst_ref=dst,
        send_sem=send_sem,
        recv_sem=recv_sem,
        device_id=device,
        device_id_type=pl.DeviceIdType.MESH,
    )


def tile_of(size, most):
    fits = [n for n in range(128, min(size, most) + 1, 128) if size % n == 0]
    return max(fits) if fits else size


class Tiles:
    def __init__(self, ref, row, col, rows, cols, lead, down):
        self.ref, self.row, self.col, self.rows, self.cols, self.lead, self.down = (
            ref, row, col, rows, cols, lead, down
        )

    def view(self, *index):
        flat, span = 0, 1
        for size, place in zip(self.lead, index):
            flat = flat * size + place
        for size in self.lead[len(index) :]:
            flat, span = flat * size, span * size
        if self.down:
            tall = self.rows * span
            start = flat * self.rows if isinstance(flat, int) else pl.multiple_of(flat * self.rows, self.rows)
            return self.ref.at[pl.ds(self.row + start, tall), pl.ds(self.col, self.cols)]
        start = flat * self.cols if isinstance(flat, int) else pl.multiple_of(flat * self.cols, self.cols)
        return self.ref.at[pl.ds(self.row, self.rows), pl.ds(self.col + start, self.cols * span)]

    def __getitem__(self, index):
        return self.view(*(index if isinstance(index, tuple) else (index,)))[...]

    def __setitem__(self, index, value):
        self.view(*(index if isinstance(index, tuple) else (index,)))[...] = value

    def clear(self):
        whole = self.view()
        whole[...] = jnp.zeros(whole.shape, whole.dtype)

    @property
    def at(self):
        return Views(self)


class Views:
    def __init__(self, tiles):
        self.tiles = tiles

    def __getitem__(self, index):
        return self.tiles.view(*(index if isinstance(index, tuple) else (index,)))


def spot_of(spot, w_down, gate, up):
    return ((w_down, gate, up)[spot[0]],) + spot[1:]


def plan_of(rows, width, half, columns, count):
    outers, quarter = count // 2, width // 2
    heads = quarter // HD
    lead = (heads // TOGETHER, TOGETHER)
    side = columns % 128 == 0
    right, below = width, 4 * rows
    lower = below + outers * 2 * rows
    flat = (rows, width, (1,), True)
    state = (HD, HD, lead, True)
    pair = (rows, columns, (outers, 2), True)
    line = (rows, columns, (outers,), True)
    plan = [(flat, (0, i * rows, 0)) for i in range(4)]
    plan.append(((rows, half, (1,), True), (0, lower, 0)))
    plan.append(((quarter, columns, (2,), True), (0, 0, right)))
    plan += [(state, (0, below, quarter + i * HD)) for i in range(7)]
    plan.append(((rows, quarter, (outers, 2), True), (0, below, 0)))
    plan += [(pair, (0, i * outers * 2 * rows, right + columns)) for i in range(2)]
    plan += [(line, (0, lower + rows, i * columns)) for i in range(4)]
    plan.append(((rows, HD, (2 * heads,), False), (1, 0, 0)))
    plan.append(((HD, HD, lead, False), (2, 0, 0)))
    plan += [((rows, columns, (outers,), not side), (2 - i, rows, 0)) for i in range(2)]
    return plan


def extent(shape, spot):
    rows, cols, lead, down = shape
    size = 1
    for n in lead:
        size = size * n
    tall, long = (rows * size, cols) if down else (rows, cols * size)
    return tall, long, spot[1] + tall, spot[2] + long


def layer_kernel(
    count,
    plan,
    query_hbm,
    keys_hbm,
    values_hbm,
    weight_hbm,
    resid_hbm,
    head_gain_ref,
    gain_ref,
    routes_ref,
    route_weights_ref,
    gate_hbm,
    up_hbm,
    down_hbm,
    mixed_ref,
    packed_ref,
    high_ref,
    low_ref,
    square_give,
    square_got,
    pages,
    x,
    gate,
    up,
    active,
    w_gate,
    w_up,
    w_down,
    mine,
    theirs,
    part,
    back,
    send_sem,
    recv_sem,
    pair_send,
    pair_recv,
    part_send,
    part_recv,
    home_send,
    home_recv,
    gate_sem,
    up_sem,
    down_sem,
    own_sem,
    load_sem,
    swap_send,
    swap_recv,
    chain_send,
    chain_recv,
    first_send,
    first_recv,
    w_send,
    w_recv,
    a_send,
    a_recv,
    pass_send,
    give_send,
    give_recv,
    cross_send,
    cross_recv,
    mhome_send,
    mhome_recv,
    square_send,
    square_recv,
    *extras,
):
    me, head = lax.axis_index("seq"), lax.axis_index("head")
    cap, half = packed_ref.shape[1], packed_ref.shape[2]
    chips = count // packed_ref.shape[0]
    chunks, wide = pages.shape[1], pages.shape[4]
    hidden = active.shape[1]
    tile = tile_of(hidden, 2304)
    group = 4
    span = group * cap

    def start_row(side, chunk):
        return pl.multiple_of(jnp.where(side == 0, head, 1 - head) * half + chunk * wide, wide)

    def weights(side, chunk):
        ks = pl.ds(start_row(side, chunk), wide)
        spot = chunk * 2 + side
        return (
            pltpu.make_async_copy(gate_hbm.at[ks], w_gate.at[ks], gate_sem.at[spot]),
            pltpu.make_async_copy(up_hbm.at[ks], w_up.at[ks], up_sem.at[spot]),
        )

    down = pltpu.make_async_copy(down_hbm, w_down, down_sem)

    def fetch(spot, carry):
        for copy in weights(lax.rem(spot, 2), spot // 2):
            copy.start()
        return carry

    def prefetch():
        lax.fori_loop(0, 2 * chunks, fetch, 0)

    (
        query,
        keys,
        values,
        normed,
        resid,
        weight,
        swap_give,
        swap_got,
        chain_got,
        chain_give,
        first_give,
        first_got,
        before,
        held,
        give,
        got,
        cross_give,
        cross_got,
        home_give,
        home,
        inside,
        own_state,
        acc_mine,
        acc_other,
    ) = (
        Tiles(*(spot if extra is None else (extra, 0, 0)), *shape)
        for extra, (shape, spot) in zip(
            extras or [None] * len(plan), ((shape, spot_of(spot, w_down, gate, up)) for shape, spot in plan)
        )
    )
    query, keys, values, normed, resid = (tiles.view(0) for tiles in (query, keys, values, normed, resid))

    outer, inner = me // 2, lax.rem(me, 2)
    outers = count // 2
    partner = outer * 2 + (1 - inner)
    rows, width = query_hbm.shape
    quarter = width // 2
    heads = quarter // HD
    together = TOGETHER
    groups = heads // together
    same = head == inner
    cross = jnp.logical_not(same)
    kept = outers // 2
    target_head = outer // kept
    f32, bf16 = jnp.float32, jnp.bfloat16

    loads = [
        pltpu.make_async_copy(src, dst, load_sem.at[i])
        for i, (src, dst) in enumerate(
            ((keys_hbm, keys), (values_hbm, values), (query_hbm, query), (resid_hbm, resid))
        )
    ]
    for load in loads:
        load.start()

    barrier = pltpu.get_barrier_semaphore()

    def greet(**device):
        pl.semaphore_signal(barrier, inc=1, device_id=device, device_id_type=pl.DeviceIdType.MESH)

    def greet_column(step, carry):
        other = lax.rem(outer + step, outers) * 2 + inner
        greet(seq=other)
        greet(seq=other, head=1 - head)
        return carry

    def greet_rest(step, carry):
        other = lax.rem(outer + step, outers) * 2 + 1 - inner
        greet(seq=other)
        return carry

    lax.fori_loop(1, outers, greet_column, 0)
    lax.fori_loop(1, outers, greet_rest, 0)
    greet(head=1 - head)
    greet(seq=partner)
    greet(seq=partner, head=1 - head)

    def lanes_of(n):
        return pl.ds(pl.multiple_of(n * HD, HD), HD)

    def state(n):
        return lax.dot_general(
            keys[:, lanes_of(n)],
            values[:, lanes_of(n)],
            (((0,), (0,)), ((), ())),
            preferred_element_type=f32,
        )

    loads[0].wait()
    loads[1].wait()

    def other_states(g, carry):
        for i in range(together):
            swap_give[g, i] = state((1 - inner) * heads + g * together + i).astype(bf16)
        return carry

    lax.fori_loop(0, groups, other_states, 0)
    pl.semaphore_wait(barrier, 3 * outers)

    def swap(g):
        return send_to(swap_give.at[g], swap_got.at[g], swap_send.at[g], swap_recv.at[g], seq=partner)

    def chain(g):
        return send_to(chain_give.at[g], chain_got.at[g], chain_send.at[g], chain_recv.at[g], seq=me + 2)

    def first(g):
        return send_to(first_give.at[g], first_got.at[g], first_send.at[g], first_recv.at[g], seq=partner)

    def post(g, carry):
        swap(g).start()
        return carry

    lax.fori_loop(0, groups, post, 0)
    prefetch()

    def cut(which):
        return pl.ds(pl.multiple_of(which * quarter, quarter), quarter)

    w_local = pltpu.make_async_copy(weight_hbm.at[cut(head)], weight.at[inner], w_recv.at[0])
    w_near = send_to(
        weight_hbm.at[cut(1 - head)], weight.at[inner], w_send.at[1], w_recv.at[0], head=1 - head
    )
    w_straight = send_to(
        weight_hbm.at[cut(head)], weight.at[inner], w_send.at[0], w_recv.at[1], seq=partner
    )
    w_turned = send_to(
        weight_hbm.at[cut(1 - head)],
        weight.at[inner],
        w_send.at[1],
        w_recv.at[1],
        seq=partner,
        head=1 - head,
    )

    @pl.when(same)
    def _():
        w_local.start()
        w_near.start()

    def own_states(g, carry):
        for i in range(together):
            own_state[g, i] = state(inner * heads + g * together + i)
        return carry

    lax.fori_loop(0, groups, own_states, 0)
    loads[2].wait()
    token = lax.broadcasted_iota(jnp.int32, (rows, rows), 0)
    causal = token >= lax.broadcasted_iota(jnp.int32, (rows, rows), 1)

    def within(n):
        scores = lax.dot_general(
            query[:, lanes_of(n)],
            keys[:, lanes_of(n)],
            (((1,), (1,)), ((), ())),
            preferred_element_type=f32,
        )
        masked = jnp.where(causal, scores, 0.0).astype(bf16)
        inside[n] = jnp.dot(masked, values[:, lanes_of(n)], preferred_element_type=f32)

    def link(g, carry):
        swap(g).wait_recv()

        @pl.when(outer > 0)
        def _():
            chain(g).wait_recv()

        for i in range(together):
            start = jnp.where(outer > 0, chain_got[g, i].astype(f32), 0.0)
            mine, theirs = own_state[g, i], swap_got[g, i].astype(f32)
            chain_give[g, i] = (start + mine + theirs).astype(bf16)
            first_give[g, i] = (start + jnp.where(inner == 0, mine, 0.0)).astype(bf16)
            before[g, i] = (start + jnp.where(inner == 1, theirs, 0.0)).astype(bf16)

        @pl.when(outer + 1 < outers)
        def _():
            chain(g).start()

        first(g).start()
        for i in range(2 * together):
            within(g * 2 * together + i)
        return carry

    @pl.when(outer == 0)
    def _():
        chain_got.clear()

    lax.fori_loop(0, groups, link, 0)

    def attend(n, prefix):
        attention = inside[n] + jnp.dot(query[:, lanes_of(n)], prefix, preferred_element_type=f32)
        scale = lax.rsqrt(jnp.mean(attention * attention, axis=-1, keepdims=True) + EPS)
        normed[:, lanes_of(n)] = (attention * scale * head_gain_ref[:, lanes_of(n)]).astype(bf16)

    def attend_first(g, carry):
        for i in range(together):
            attend(inner * heads + g * together + i, before[g, i])
        return carry

    lax.fori_loop(0, groups, attend_first, 0)

    def a_remote(which, recv, **device):
        return send_to(
            normed.at[:, cut(which)], held.at[outer, inner], a_send.at[0], a_recv.at[outer, inner], **device
        )

    a_local = pltpu.make_async_copy(
        normed.at[:, cut(inner)], held.at[outer, inner], a_recv.at[outer, inner]
    )
    a_turned = a_remote(inner, 1, seq=partner, head=1 - head)
    a_near = send_to(
        normed.at[:, cut(1 - inner)],
        held.at[outer, inner],
        a_send.at[1],
        a_recv.at[outer, inner],
        head=1 - head,
    )
    a_straight = send_to(
        normed.at[:, cut(1 - inner)],
        held.at[outer, inner],
        a_send.at[1],
        a_recv.at[outer, inner],
        seq=partner,
    )

    @pl.when(same)
    def _():
        a_local.start()

    @pl.when(cross)
    def _():
        a_turned.start()

    def attend_second(g, carry):
        first(g).wait_recv()
        for i in range(together):
            attend((1 - inner) * heads + g * together + i, first_got[g, i])
        return carry

    lax.fori_loop(0, groups, attend_second, 0)

    @pl.when(same)
    def _():
        a_near.start()

    @pl.when(cross)
    def _():
        a_straight.start()
        w_straight.start()
        w_turned.start()

    experts_count = packed_ref.shape[0]
    places = high_ref.shape[0]
    expert = lax.broadcasted_iota(jnp.int32, (16, rows), 0)
    names = [routes_ref[j : j + 1, :] for j in range(TOP)]
    marks = sum((expert == name).astype(f32) for name in names)
    later = (token < lax.broadcasted_iota(jnp.int32, (rows, rows), 1)).astype(bf16)
    ahead = jnp.dot(marks.astype(bf16), later, preferred_element_type=f32)
    slots = [
        jnp.sum(jnp.where(expert == name, ahead, 0.0), axis=0, keepdims=True).astype(jnp.int32)
        for name in names
    ]
    place = lax.broadcasted_iota(jnp.int32, (places, rows), 0)
    factors = jnp.zeros((places, rows), f32)
    for j in range(TOP):
        for chip in range(chips):
            hit = place == (names[j] * chips + chip) * cap + slots[j]
            factors = factors + jnp.where(hit, route_weights_ref[j : j + 1, :], 0.0)
    high = factors.astype(bf16)
    high_ref[...] = high
    low_ref[...] = (factors - high.astype(f32)).astype(bf16)

    def move(source, side, up):
        return send_to(
            held.at[source, side],
            held.at[source, side],
            pass_send.at[source, side, up],
            a_recv.at[source, side],
            seq=me + (2 if up else -2),
        )

    def forward(source, side):
        @pl.when((source <= outer) & (outer + 1 < outers))
        def _():
            move(source, side, 1).start()

        @pl.when((source >= outer) & (outer > 0))
        def _():
            move(source, side, 0).start()

    def arrive(source):
        for turn in range(2):
            side = head if turn == 0 else 1 - head
            move(source, side, 0).wait_recv()
            forward(source, side)

    def own_near():
        @pl.when(same)
        def _():
            a_local.wait()

        @pl.when(cross)
        def _():
            a_near.wait_recv()

        forward(outer, inner)

    def own_far():
        send_to(
            normed.at[:, cut(0)], held.at[outer, 1 - inner], a_send.at[0], a_recv.at[outer, 1 - inner], seq=partner
        ).wait_recv()
        forward(outer, 1 - inner)

    @pl.when(same)
    def _():
        own_near()
        own_far()

    @pl.when(cross)
    def _():
        own_far()
        own_near()

    def hand(source):
        return send_to(give.at[source], got.at[source], give_send.at[source], give_recv.at[source], head=1 - head)

    def over(source):
        return send_to(
            cross_give.at[source], cross_got.at[source], cross_send.at[source], cross_recv.at[source], seq=partner
        )

    spot = lax.rem(outer, kept) * 2 + head

    def home_to(source):
        return send_to(
            home_give.at[source],
            home.at[spot],
            mhome_send.at[source],
            mhome_recv.at[spot],
            seq=source * 2 + inner,
            head=target_head,
        )

    home_own = pltpu.make_async_copy(home_give.at[outer], home.at[spot], mhome_recv.at[spot])
    stays = head == target_head

    def multiply(source):
        block = held[source]
        give[source] = jnp.dot(block, weight[1 - head], preferred_element_type=f32).astype(bf16)
        hand(source).start()
        both = jnp.dot(block, weight[head], preferred_element_type=f32)
        acc_mine[source] = jnp.where(inner == 0, both[:rows], both[rows:])
        acc_other[source] = jnp.where(inner == 0, both[rows:], both[:rows])

    def reduce_pair(source):
        hand(source).wait_recv()
        cross_give[source] = (
            acc_other[source] + got[source, 1 - inner].astype(f32)
        ).astype(bf16)
        over(source).start()
        acc_mine[source] = acc_mine[source] + got[source, inner].astype(f32)

    def send_home(source):
        over(source).wait_recv()
        home_give[source] = (acc_mine[source] + cross_got[source].astype(f32)).astype(bf16)

        @pl.when((source == outer) & stays)
        def _():
            home_own.start()

        @pl.when(jnp.logical_not((source == outer) & stays))
        def _():
            home_to(source).start()

    def near(distance, action):
        @pl.when((outer - distance >= 0) & (distance > 0))
        def _():
            action(outer - distance)

        @pl.when(outer + distance < outers)
        def _():
            action(outer + distance)

    near(1, arrive)

    @pl.when(same)
    def _():
        w_local.wait()

    @pl.when(cross)
    def _():
        w_near.wait_recv()

    send_to(
        weight_hbm.at[cut(0)], weight.at[1 - inner], w_send.at[0], w_recv.at[1], seq=partner
    ).wait_recv()
    multiply(outer)
    near(1, multiply)
    reduce_pair(outer)
    near(1, reduce_pair)
    send_home(outer)

    def step(distance, carry):
        near(distance, arrive)
        near(distance, multiply)
        near(distance - 1, send_home)
        near(distance, reduce_pair)
        return carry

    lax.fori_loop(2, outers, step, 0)
    near(outers - 1, send_home)

    def collect(piece, carry):
        source = head * kept + piece // 2
        local = (source == outer) & (lax.rem(piece, 2) == head)

        @pl.when(local)
        def _():
            home_own.wait()

        @pl.when(jnp.logical_not(local))
        def _():
            send_to(
                home_give.at[0], home.at[piece], mhome_send.at[0], mhome_recv.at[piece], head=1 - head
            ).wait_recv()

        return carry

    lax.fori_loop(0, 2 * kept, collect, 0)
    loads[3].wait()
    projected = jnp.concatenate([home[piece].astype(f32) for piece in range(2 * kept)], axis=1)
    stream = (projected + resid[...].astype(f32)).astype(bf16)
    mixed_ref[...] = stream
    broad = stream.astype(f32)
    square = jnp.sum(broad * broad, axis=1, keepdims=True)
    square_give[...] = jnp.broadcast_to(square, square_give.shape)
    trade = send_to(square_give, square_got, square_send, square_recv, head=1 - head)
    trade.start()
    pick = lax.broadcasted_iota(jnp.int32, (experts_count * cap, rows), 0)
    picker = sum((pick == names[j] * cap + slots[j]).astype(f32) for j in range(TOP)).astype(bf16)
    trade.wait_recv()
    scale = lax.rsqrt((square + square_got[:, 0:1]) / (2 * half) + EPS)
    gain = gain_ref[:, pl.ds(pl.multiple_of(head * half, half), half)]
    moe_in = (broad * scale * gain).astype(bf16)
    chosen = jnp.dot(picker, moe_in, preferred_element_type=f32)
    for page in range(experts_count):
        packed_ref[page] = chosen[page * cap : (page + 1) * cap].astype(bf16)

    trade.wait_send()

    @pl.when(same)
    def _():
        w_near.wait_send()
        a_near.wait_send()

    @pl.when(cross)
    def _():
        w_straight.wait_send()
        w_turned.wait_send()
        a_turned.wait_send()
        a_straight.wait_send()

    def finish_group(g, carry):
        swap(g).wait_send()
        first(g).wait_send()

        @pl.when(outer + 1 < outers)
        def _():
            chain(g).wait_send()

        return carry

    lax.fori_loop(0, groups, finish_group, 0)

    def finish(source, carry):
        hand(source).wait_send()
        over(source).wait_send()

        @pl.when(jnp.logical_not((source == outer) & stays))
        def _():
            home_to(source).wait_send()

        for side in range(2):

            @pl.when((source <= outer) & (outer + 1 < outers))
            def _():
                move(source, side, 1).wait_send()

            @pl.when((source >= outer) & (outer > 0))
            def _():
                move(source, side, 0).wait_send()

        return carry

    lax.fori_loop(0, outers, finish, 0)

    down.start()

    def chunk_of(chunk):
        return pl.ds(pl.multiple_of(chunk * wide, wide), wide)

    def out(chunk, other):
        return send_to(
            packed_ref.at[other // chips, :, chunk_of(chunk)],
            pages.at[0, chunk, me],
            send_sem.at[chunk, other],
            recv_sem.at[chunk, me],
            seq=other,
        )

    def arrival(chunk, other):
        return send_to(
            packed_ref.at[other // chips, :, chunk_of(chunk)],
            pages.at[0, chunk, other],
            send_sem.at[chunk, other],
            recv_sem.at[chunk, other],
            seq=other,
        )

    def keep(chunk):
        return pltpu.make_async_copy(
            packed_ref.at[me // chips, :, chunk_of(chunk)], pages.at[0, chunk, me], own_sem.at[chunk]
        )

    def pair_copy(chunk):
        return send_to(
            pages.at[0, chunk], pages.at[1, chunk], pair_send.at[chunk], pair_recv.at[chunk], head=1 - head
        )

    def post(chunk, carry):
        def one(step, inside):
            out(chunk, lax.rem(me + step, count)).start()
            return inside

        lax.fori_loop(1, count, one, 0)
        keep(chunk).start()
        return carry

    lax.fori_loop(0, chunks, post, 0)
    gate[...] = jnp.zeros_like(gate)
    up[...] = jnp.zeros_like(up)

    def join(pages):
        return jnp.concatenate([page.astype(jnp.float32) for page in pages], axis=0).astype(jnp.bfloat16)

    def gather(side, chunk):
        def one(g, carry):
            x[pl.ds(pl.multiple_of(g * span, 16), span), :] = join(
                [pages[side, chunk, g * group + i] for i in range(group)]
            )
            return carry

        lax.fori_loop(0, count // group, one, 0)

    def accumulate(side, chunk):
        for copy in weights(side, chunk):
            copy.wait()
        gather(side, chunk)
        ks = pl.ds(start_row(side, chunk), wide)

        def one(n, carry):
            cols = pl.ds(pl.multiple_of(n * tile, tile), tile)
            gate[:, cols] += jnp.dot(x[...], w_gate[ks, cols], preferred_element_type=jnp.float32)
            up[:, cols] += jnp.dot(x[...], w_up[ks, cols], preferred_element_type=jnp.float32)
            return carry

        lax.fori_loop(0, hidden // tile, one, 0)

    def take(chunk, carry):
        def one(step, inside):
            arrival(chunk, lax.rem(me + count - step, count)).wait_recv()
            return inside

        lax.fori_loop(1, count, one, 0)
        keep(chunk).wait()
        pair_copy(chunk).start()
        accumulate(0, chunk)
        pair_copy(chunk).wait_recv()
        accumulate(1, chunk)
        return carry

    lax.fori_loop(0, chunks, take, 0)

    small = tile_of(hidden, 256)

    def activate(n, carry):
        cols = pl.ds(pl.multiple_of(n * small, small), small)
        active[:, cols] = (jax.nn.silu(gate[:, cols]) * up[:, cols]).astype(jnp.bfloat16)
        return carry

    lax.fori_loop(0, hidden // small, activate, 0)
    down.wait()

    def hand_part(chunk):
        return send_to(mine.at[chunk], theirs.at[chunk], part_send.at[chunk], part_recv.at[chunk], head=1 - head)

    def back_home(chunk, other):
        return send_to(
            mine.at[chunk, other],
            back.at[chunk, me],
            home_send.at[chunk, other],
            home_recv.at[chunk, me],
            seq=other,
        )

    def home_arrival(chunk, other):
        return send_to(
            mine.at[chunk, other],
            back.at[chunk, other],
            home_send.at[chunk, other],
            home_recv.at[chunk, other],
            seq=other,
        )

    def project(side, chunk):
        cols = pl.ds(start_row(side, chunk), wide)
        part[...] = jnp.dot(active[...], w_down[:, cols], preferred_element_type=jnp.float32)

    def give(chunk, carry):
        project(1, chunk)

        def split(g, inside):
            block = part[pl.ds(pl.multiple_of(g * span, 8), span), :]
            for i in range(group):
                mine[chunk, g * group + i] = block[i * cap : (i + 1) * cap].astype(jnp.bfloat16)
            return inside

        lax.fori_loop(0, count // group, split, 0)
        hand_part(chunk).start()
        project(0, chunk)
        hand_part(chunk).wait_recv()
        hand_part(chunk).wait_send()

        def add(g, inside):
            block = part[pl.ds(pl.multiple_of(g * span, 8), span), :]
            for i in range(group):
                spot = g * group + i
                mine[chunk, spot] = (
                    block[i * cap : (i + 1) * cap] + theirs[chunk, spot].astype(jnp.float32)
                ).astype(jnp.bfloat16)
            return inside

        lax.fori_loop(0, count // group, add, 0)

        def one(step, inside):
            back_home(chunk, lax.rem(me + step, count)).start()
            return inside

        lax.fori_loop(1, count, one, 0)
        back[chunk, me] = mine[chunk, me]
        return carry

    lax.fori_loop(0, chunks, give, 0)

    rows_of = (((0,), (0,)), ((), ()))

    def mix(chunk, carry):
        def one(step, inside):
            home_arrival(chunk, lax.rem(me + count - step, count)).wait_recv()
            return inside

        lax.fori_loop(1, count, one, 0)

        def pack(g, inside):
            x[pl.ds(pl.multiple_of(g * span, 16), span), :] = join(
                [back[chunk, g * group + i] for i in range(group)]
            )
            return inside

        lax.fori_loop(0, count // group, pack, 0)
        cols = chunk_of(chunk)
        mixed_ref[:, cols] = (
            mixed_ref[:, cols].astype(jnp.float32)
            + lax.dot_general(high_ref[...], x[...], rows_of, preferred_element_type=jnp.float32)
            + lax.dot_general(low_ref[...], x[...], rows_of, preferred_element_type=jnp.float32)
        ).astype(jnp.bfloat16)
        return carry

    lax.fori_loop(0, chunks, mix, 0)

    def finish_all(chunk, carry):
        def one(step, inside):
            other = lax.rem(me + step, count)
            out(chunk, other).wait_send()
            back_home(chunk, other).wait_send()
            return inside

        lax.fori_loop(1, count, one, 0)
        pair_copy(chunk).wait_send()
        return carry

    lax.fori_loop(0, chunks, finish_all, 0)


def layer(query, keys, values, out_weight, resid, attn_gain, moe_gain, routes, route_weights, w_gate, w_up, w_down):
    count = lax.axis_size("seq")
    outers = count // 2
    rows, width = query.shape
    columns = out_weight.shape[1]
    half = resid.shape[1]
    groups = width // HD // 2 // TOGETHER
    hidden = w_gate.shape[1]
    wide = tile_of(half, 512)
    chunks = half // wide
    slots = count * CAP
    pages = (chunks, count, CAP, wide)
    dma = pltpu.SemaphoreType.DMA
    vmem = pl.BlockSpec(memory_space=pltpu.VMEM)
    hbm = pl.BlockSpec(memory_space=pltpu.HBM)
    bf16, f32 = jnp.bfloat16, jnp.float32
    plan = plan_of(rows, width, half, columns, count)
    room = (w_down.shape, (slots, hidden), (slots, hidden))
    shared = columns % 128 == 0 and all(
        extent(shape, spot)[2] <= room[spot[0]][0] and extent(shape, spot)[3] <= room[spot[0]][1]
        for shape, spot in plan
    )
    extras = [
        pltpu.VMEM(extent(shape, spot)[:2], f32 if spot[0] else bf16) for shape, spot in plan if not shared
    ]
    return pl.pallas_call(
        functools.partial(layer_kernel, count, plan),
        name="layer",
        out_shape=jax.ShapeDtypeStruct((rows, half), bf16),
        in_specs=[hbm] * 5 + [vmem] * 4 + [hbm] * 3,
        out_specs=vmem,
        scratch_shapes=[
            pltpu.VMEM((EXPERTS, CAP, half), bf16),
            pltpu.VMEM((slots, rows), bf16),
            pltpu.VMEM((slots, rows), bf16),
            pltpu.VMEM((rows, 128), f32),
            pltpu.VMEM((rows, 128), f32),
            pltpu.VMEM((2,) + pages, bf16),
            pltpu.VMEM((slots, wide), bf16),
            pltpu.VMEM((slots, hidden), f32),
            pltpu.VMEM((slots, hidden), f32),
            pltpu.VMEM((slots, hidden), bf16),
            pltpu.VMEM(w_gate.shape, bf16),
            pltpu.VMEM(w_up.shape, bf16),
            pltpu.VMEM(w_down.shape, bf16),
            pltpu.VMEM(pages, bf16),
            pltpu.VMEM(pages, bf16),
            pltpu.VMEM((slots, wide), f32),
            pltpu.VMEM(pages, bf16),
            dma((chunks, count)),
            dma((chunks, count)),
            dma((chunks,)),
            dma((chunks,)),
            dma((chunks,)),
            dma((chunks,)),
            dma((chunks, count)),
            dma((chunks, count)),
            dma((2 * chunks,)),
            dma((2 * chunks,)),
            dma,
            dma((chunks,)),
            dma((4,)),
            dma((groups,)),
            dma((groups,)),
            dma((groups,)),
            dma((groups,)),
            dma((groups,)),
            dma((groups,)),
            dma((2,)),
            dma((2,)),
            dma((2,)),
            dma((outers, 2)),
            dma((outers, 2, 2)),
            dma((outers,)),
            dma((outers,)),
            dma((outers,)),
            dma((outers,)),
            dma((outers,)),
            dma((outers,)),
            dma,
            dma,
        ]
        + extras,
        compiler_params=pltpu.CompilerParams(
            collective_id=0, has_side_effects=True, vmem_limit_bytes=VMEM_MOST
        ),
    )(
        query,
        keys,
        values,
        out_weight,
        resid,
        attn_gain.reshape(1, width),
        moe_gain.reshape(1, 2 * half),
        routes.T,
        route_weights.T,
        w_gate,
        w_up,
        w_down,
    )


def per_device(
    query,
    keys,
    values,
    resid,
    attn_gain,
    out_weight,
    moe_gain,
    routes,
    route_weights,
    w_gate,
    w_up,
    w_down,
):
    return layer(
        query,
        keys,
        values,
        out_weight,
        resid,
        attn_gain,
        moe_gain,
        routes,
        route_weights,
        w_gate,
        w_up,
        w_down,
    )


def solution(mesh):
    return jax.shard_map(
        per_device,
        mesh=mesh,
        in_specs=(
            P(("grp", "seq"), "head"),
            P(("grp", "seq"), "head"),
            P(("grp", "seq"), "head"),
            P(("grp", "seq"), "head"),
            P("head"),
            P("head", "seq"),
            P(),
            P(("grp", "seq"), None),
            P(("grp", "seq"), None),
            P(None, ("seq", "head")),
            P(None, ("seq", "head")),
            P(("seq", "head"), None),
        ),
        out_specs=P(("grp", "seq"), "head"),
        check_vma=False,
    )
```
